256 devices in a mesh: cell: 8 (over y, z_hi), gene: 32 (over x, z_lo, core).
Axes of the slice: x: 4, y: 4, z: 8 (z_hi: 2, z_lo: 4; z = z_hi * 4 + z_lo), core: 2. Of those that a mesh axis runs over, the one named last changes fastest.
Arguments:
- blocks: bfloat16 [12288, 256, 256], P(('cell', 'gene')), may hold values from 0 to 255, as said below
- block_rows: int32 [12288], P(('cell', 'gene')), may hold values from 0 to 15, as said below
- block_cols: int32 [12288], P(('cell', 'gene')), may hold values from 0 to 3, as said below
- block_count: int32 [256], P(('cell', 'gene')), may hold values from 2 to 48, as said below
- cell_factor: float32 [32768, 128], P(('cell', 'gene')), as said below
- gene_factor: float32 [32768, 128], P('gene'), as said below
Outputs:
- cell_new: float32 [32768, 128], P(('cell', 'gene'))
- gene_new: float32 [32768, 128], P('gene')
The draws below stay inside these ranges and needn't reach their ends.
Inputs may be any that keep to these rules, and one draw needn't show every extreme that they name: `blocks`: counts are whole numbers. `block_rows`: within one device the live slots and the padding slots name distinct block positions. `block_cols`: within one device the live slots and the padding slots name distinct block positions. `block_count`: some device has all 48 slots live. `cell_factor`: positive entries. `gene_factor`: positive entries.
All inputs are finite; a program needn't handle non-finite values.
Results may differ from the reference program's by a relative error of at most 0.00084.
Values may be sent and summed in bfloat16 or wider, within the bound.
No kernel may reach another device: no remote copies, remote signals or barrier semaphores. Data moves between devices by JAX's collectives and lax.ppermute only.
A program may use at most 64 MiB of HBM per device.

```python
import jax
import jax.numpy as jnp
from jax import lax

BLK = 256
R = 128
GENE_DEV = 1024
CELL_DEV = 4096
NB_DEV = 48
CELLS = 32768
GENES = 32768
N_CELL = 8
N_GENE = 32


def positions(key):
    devs = N_CELL * N_GENE
    keys = jax.random.split(jax.random.fold_in(key, 7), devs)
    total = CELL_DEV // BLK * (GENE_DEV // BLK)
    picked = jax.vmap(lambda one: jax.random.permutation(one, total)[:NB_DEV])(keys)
    return picked.reshape(-1).astype(jnp.int32)


def draw_block_rows(key, part):
    return (positions(key) // (GENE_DEV // BLK)).astype(jnp.int32)


def draw_block_cols(key, part):
    return (positions(key) % (GENE_DEV // BLK)).astype(jnp.int32)


def draw_block_count(key, part):
    devs = N_CELL * N_GENE
    first_key = jax.random.fold_in(key, 21)
    second_key = jax.random.fold_in(key, 22)
    third_key = jax.random.fold_in(key, 23)
    left = jax.random.randint(first_key, (devs,), 0, NB_DEV - 1)
    right = jax.random.randint(second_key, (devs,), 0, NB_DEV - 1)
    counts = 2 + left * right // (NB_DEV - 2)
    fullest = jax.random.randint(third_key, (), 0, devs)
    return jnp.where(jnp.arange(devs) == fullest, NB_DEV, counts).astype(jnp.int32)


def draw_blocks(key, part):
    shape = (N_CELL * N_GENE * NB_DEV, BLK, BLK)
    inner = jax.random.fold_in(key, 3)
    values = jax.random.randint(inner, shape, 0, 256)
    return values.astype(jnp.float32).astype(jnp.bfloat16)


def factor_draw(key, count):
    base_key = jax.random.fold_in(key, 41)
    rank_key = jax.random.fold_in(key, 42)
    boost_key = jax.random.fold_in(key, 43)
    rising = 1.0 + 2.0 * jnp.arange(count, dtype=jnp.float32)[:, None] / count
    leading = max(1, R // 32)
    chosen_ranks = jax.random.randint(rank_key, (count, leading), 0, R)
    ranks = jnp.arange(R, dtype=jnp.int32)[None, :]
    marked = jnp.zeros((count, R), jnp.float32)
    for which in range(leading):
        marked = jnp.maximum(marked, (chosen_ranks[:, which:which + 1] == ranks).astype(jnp.float32))
    base = jnp.exp(jax.random.uniform(base_key, (count, R), jnp.float32, jnp.log(0.05), jnp.log(0.5)))
    boost = jnp.exp(jax.random.uniform(boost_key, (count, R), jnp.float32, jnp.log(3.0), jnp.log(12.0)))
    entries = jnp.where(marked > 0.0, boost, base)
    return (entries * rising).astype(jnp.float32)


def draw_cell_factor(key, part):
    return factor_draw(jax.random.fold_in(key, 51), CELLS)


def draw_gene_factor(key, part):
    return factor_draw(jax.random.fold_in(key, 52), GENES)


def setup_inputs(seed: int = 0) -> dict:
    arg_keys = jax.random.split(jax.random.key(seed), 7)
    blocks = draw_blocks(jax.random.fold_in(arg_keys[6], 71), 0)
    block_rows = draw_block_rows(jax.random.fold_in(arg_keys[6], 71), 0)
    block_cols = draw_block_cols(jax.random.fold_in(arg_keys[6], 71), 0)
    block_count = draw_block_count(jax.random.fold_in(arg_keys[6], 71), 0)
    cell_factor = draw_cell_factor(jax.random.fold_in(arg_keys[6], 71), 0)
    gene_factor = draw_gene_factor(jax.random.fold_in(arg_keys[6], 71), 0)
    return dict(blocks=blocks, block_rows=block_rows, block_cols=block_cols, block_count=block_count, cell_factor=cell_factor, gene_factor=gene_factor)


def block_ratio(tiles, row_tiles, col_tiles, live):
    model = jnp.einsum('nir,njr->nij', row_tiles.astype(jnp.float32), col_tiles.astype(jnp.float32))
    return (tiles.astype(jnp.float32) / model * live[:, None, None]).astype(jnp.bfloat16)


def reference(blocks, block_rows, block_cols, block_count, cell_factor, gene_factor):
    devs = N_CELL * N_GENE
    row_blocks = CELL_DEV // BLK
    col_blocks = GENE_DEV // BLK
    tiles = blocks.reshape(devs, NB_DEV, BLK, BLK)
    rows = block_rows.reshape(devs, NB_DEV).astype(jnp.int32)
    cols = block_cols.reshape(devs, NB_DEV).astype(jnp.int32)
    counts = block_count.astype(jnp.int32)
    order = jnp.arange(devs, dtype=jnp.int32)
    cell_bf = cell_factor.astype(jnp.bfloat16)
    gene_bf = gene_factor.astype(jnp.bfloat16)

    def prepare(cell_src, item):
        tile, row, col, count, index = item
        cstart = ((index // N_GENE) * CELL_DEV).astype(jnp.int32)
        gstart = ((index % N_GENE) * GENE_DEV).astype(jnp.int32)
        w_tile = lax.dynamic_slice_in_dim(cell_src, cstart, CELL_DEV, 0)
        h_tile = lax.dynamic_slice_in_dim(gene_bf, gstart, GENE_DEV, 0)
        live = (jnp.arange(NB_DEV, dtype=jnp.int32) < count).astype(jnp.float32)
        row_tiles = w_tile.reshape(row_blocks, BLK, R)[row]
        col_tiles = h_tile.reshape(col_blocks, BLK, R)[col]
        ratio = block_ratio(tile, row_tiles, col_tiles, live)
        return ratio, row_tiles, col_tiles, cstart, gstart

    def first(carry, item):
        ratio, row_tiles, col_tiles, cstart, gstart = prepare(cell_bf, item)
        terms = jnp.einsum('nij,njr->nir', ratio.astype(jnp.float32), col_tiles.astype(jnp.float32))
        sums = jax.ops.segment_sum(terms, item[1], num_segments=row_blocks).reshape(CELL_DEV, R)
        old = lax.dynamic_slice_in_dim(carry, cstart, CELL_DEV, 0)
        return lax.dynamic_update_slice_in_dim(carry, old + sums, cstart, 0), None

    numer_w, unused = lax.scan(first, jnp.zeros((CELLS, R), jnp.float32), (tiles, rows, cols, counts, order))
    gene_sums = jnp.sum(gene_factor, 0)
    cell_new = cell_factor * numer_w / gene_sums
    new_bf = cell_new.astype(jnp.bfloat16)

    def second(carry, item):
        ratio, row_tiles, col_tiles, cstart, gstart = prepare(new_bf, item)
        terms = jnp.einsum('nij,nir->njr', ratio.astype(jnp.float32), row_tiles.astype(jnp.float32))
        sums = jax.ops.segment_sum(terms, item[2], num_segments=col_blocks).reshape(GENE_DEV, R)
        old = lax.dynamic_slice_in_dim(carry, gstart, GENE_DEV, 0)
        return lax.dynamic_update_slice_in_dim(carry, old + sums, gstart, 0), None

    numer_h, unused = lax.scan(second, jnp.zeros((GENES, R), jnp.float32), (tiles, rows, cols, counts, order))
    cell_sums = jnp.sum(cell_new, 0)
    gene_new = gene_factor * numer_h / cell_sums
    return cell_new, gene_new
```

```python
import jax
import jax.numpy as jnp
from jax import lax
from jax.experimental import pallas as pl
from jax.experimental.pallas import tpu as pltpu
from jax.sharding import Mesh
from jax.sharding import PartitionSpec as P

GENE = ("x", "zl", "c")
CELL_GENE = ("y", "zh", "x", "zl", "c")

BLK = 256
R = 128
NB = 48
HALF = 128
PAD = 144
UNITS = 32
PAIR = 2
BF = jnp.bfloat16
F32 = jnp.float32
NT = (((1,), (1,)), ((), ()))
VMEM_LIMIT = 48 * 1024 * 1024


def shift(value, axis, step):
    count = lax.axis_size(axis)
    return lax.ppermute(value, axis, [(i, (i + step) % count) for i in range(count)])


def gathered(payload):
    for axis in ("zl", "x", "c"):
        parts = [payload] + [shift(payload, axis, k) for k in range(1, lax.axis_size(axis))]
        payload = jnp.concatenate(parts, 0)
    return payload


def three_pieces(total):
    hi = total.astype(BF)
    rest = total - hi.astype(F32)
    mid = rest.astype(BF)
    lo = (rest - mid.astype(F32)).astype(BF)
    wide = lambda a: jnp.concatenate([a.astype(F32)] * 2, 0)
    which = lax.broadcasted_iota(jnp.int32, (16, R), 0)
    rows = jnp.where(
        which == 0,
        wide(hi),
        jnp.where(which == 1, wide(mid), jnp.where(which == 2, wide(lo), 0.0)),
    )
    return rows.astype(BF)


def column_sum(value):
    return jnp.broadcast_to(jnp.sum(value, 0, keepdims=True), (8, R))


def joined(pieces):
    return column_sum(pieces.astype(F32))


def prep_kernel(cell_ref, gene_ref, pay_ref):
    pay_ref[:HALF, :] = cell_ref[...].astype(BF)
    pay_ref[HALF:, :] = three_pieces(column_sum(gene_ref[...]))


def slot_base(meta, row, parity):
    dx = (meta[0] - (row >> 2)) & 3
    dz = (meta[1] - (row & 3)) & 3
    dc = meta[2] ^ parity
    return pl.multiple_of((dc * 16 + dx * 4 + dz) * PAD, 16)


def unit_base(meta, row, parity):
    dx = ((row >> 2) - meta[0]) & 3
    dz = ((row & 3) - meta[1]) & 3
    dc = meta[2] ^ parity
    return pl.multiple_of((dc * 16 + dx * 4 + dz) * HALF, HALF)


def fetch_all(blocks_ref, tiles, sems):
    def start(s, carry):
        pltpu.make_async_copy(blocks_ref.at[s], tiles.at[s], sems.at[s]).start()
        return carry

    lax.fori_loop(0, NB, start, 0)


def await_tile(blocks_ref, tiles, sems, s):
    pltpu.make_async_copy(blocks_ref.at[s], tiles.at[s], sems.at[s]).wait()


def ratio_of(tile, w, h, live):
    model = lax.dot_general(w, h, NT, preferred_element_type=F32)
    return (tile.astype(F32) / model * live).astype(BF)


def group_sum(g_ref):
    def add(u, total):
        return total + g_ref[pl.ds(pl.multiple_of(u * PAD + HALF, 16), 16), :].astype(F32)

    total = lax.fori_loop(0, UNITS, add, jnp.zeros((16, R), F32))
    return column_sum(total)


def over_slots(count, meta, blocks_ref, tiles, sems, body):
    steps = (count + PAIR - 1) // PAIR

    def step(p, carry):
        for k in range(PAIR):
            await_tile(blocks_ref, tiles, sems, p * PAIR + k)
        for k in range(PAIR):
            body(p * PAIR + k)
        return carry

    lax.fori_loop(0, steps, step, 0)

    def drain(s, carry):
        await_tile(blocks_ref, tiles, sems, s)
        return carry

    lax.fori_loop(steps * PAIR, NB, drain, 0)


def cells_kernel(
    meta, rows, cols, blocks_ref, g_ref, gene_ref, keep_ref, send_ref, sum_ref, tiles, hb, acc, sems
):
    fetch_all(blocks_ref, tiles, sems)
    hb[...] = gene_ref[...].astype(BF)
    acc[...] = jnp.zeros_like(acc)
    sum_ref[...] = group_sum(g_ref)
    count = meta[3]

    def body(s):
        row = rows[s]
        live = jnp.where(s < count, 1.0, 0.0).astype(F32)
        h = hb[pl.ds(pl.multiple_of(cols[s] * BLK, BLK), BLK), :]
        w = jnp.concatenate(
            [g_ref[pl.ds(slot_base(meta, row, parity), HALF), :] for parity in (0, 1)], 0
        )
        ratio = ratio_of(tiles[s], w, h, live)
        terms = jnp.dot(ratio, h, preferred_element_type=F32)
        for parity in (0, 1):
            at = pl.ds(unit_base(meta, row, parity), HALF)
            acc[at, :] = acc[at, :] + terms[parity * HALF : (parity + 1) * HALF]

    over_slots(count, meta, blocks_ref, tiles, sems, body)
    half = UNITS // 2 * HALF
    keep_ref[...] = acc[:half, :]
    send_ref[...] = acc[half:, :].astype(BF)


def update_kernel(own_ref, r1_ref, r2_ref, r3_ref, cell_ref, sum_ref, new_ref, pay_ref):
    numer = own_ref[...] + r1_ref[...] + r2_ref[...] + r3_ref[...]
    new = cell_ref[...] * numer / sum_ref[0:1, :]
    new_ref[...] = new
    pay_ref[:HALF, :] = new.astype(BF)
    pay_ref[HALF:, :] = three_pieces(column_sum(new))


def genes_kernel(
    meta, rows, cols, blocks_ref, g_ref, gene_ref, own_ref, send_ref, sum_ref, tiles, hb, wt, acc, sems
):
    fetch_all(blocks_ref, tiles, sems)
    hb[...] = gene_ref[...].astype(BF)
    acc[...] = jnp.zeros_like(acc)
    total = group_sum(g_ref)
    sum_ref[...] = total
    count = meta[3]

    def load_w(row):
        return jnp.concatenate(
            [g_ref[pl.ds(slot_base(meta, row, parity), HALF), :] for parity in (0, 1)], 0
        )

    def turn(row, carry):
        wt[row] = load_w(row).T
        return carry

    lax.fori_loop(0, wt.shape[0], turn, 0)

    def body(s):
        row = rows[s]
        live = jnp.where(s < count, 1.0, 0.0).astype(F32)
        h = hb[pl.ds(pl.multiple_of(cols[s] * BLK, BLK), BLK), :]
        ratio = ratio_of(tiles[s], load_w(row), h, live)
        at = (cols[s] - meta[4]) & 3
        acc[at] = acc[at] + jnp.dot(wt[row], ratio, preferred_element_type=F32)

    over_slots(count, meta, blocks_ref, tiles, sems, body)
    own_ref[...] = acc[0].T
    pieces = three_pieces(total)
    for k in range(1, 4):
        send_ref[k - 1, :BLK, :] = acc[k].T.astype(BF)
        send_ref[k - 1, BLK:, :] = pieces


def fold_kernel(own_ref, sum_ref, r1_ref, r2_ref, r3_ref, out_ref):
    numer = own_ref[...]
    total = sum_ref[...]
    for ref in (r1_ref, r2_ref, r3_ref):
        numer = numer + ref[:BLK, :].astype(F32)
        total = total + joined(ref[BLK:, :])
    out_ref[:BLK, :] = numer
    out_ref[BLK:, :] = total


def finish_kernel(meta, mine_ref, other_ref, gene_ref, out_ref):
    both = mine_ref[...] + other_ref[...]
    at = pl.ds(pl.multiple_of(meta[4] * BLK, BLK), BLK)
    out_ref[...] = gene_ref[at, :] * both[:BLK] / both[BLK : BLK + 1]


def place_kernel(meta, p0_ref, p1_ref, p2_ref, p3_ref, out_ref):
    for k, ref in enumerate((p0_ref, p1_ref, p2_ref, p3_ref)):
        at = pl.ds(pl.multiple_of(((meta[4] - k) & 3) * BLK, BLK), BLK)
        out_ref[at, :] = ref[...]


def vspec():
    return pl.BlockSpec(memory_space=pltpu.VMEM)


def sspec():
    return pl.BlockSpec(memory_space=pltpu.SMEM)


def call(kernel, outs, args, kinds, scratch=(), name=None):
    spec = {"s": sspec, "v": vspec, "a": lambda: pl.BlockSpec(memory_space=pl.ANY)}
    return pl.pallas_call(
        kernel,
        out_shape=outs,
        in_specs=[spec[kind]() for kind in kinds],
        out_specs=jax.tree.map(lambda _: vspec(), outs),
        scratch_shapes=list(scratch),
        name=name,
        compiler_params=pltpu.CompilerParams(vmem_limit_bytes=VMEM_LIMIT),
    )(*args)


def shape(dims, dtype):
    return jax.ShapeDtypeStruct(dims, dtype)


def on_device(blocks, block_rows, block_cols, block_count, cell_factor, gene_factor):
    genes = gene_factor.shape[0]
    half = UNITS // 2 * HALF
    meta = jnp.stack(
        [
            lax.axis_index("x"),
            lax.axis_index("zl"),
            lax.axis_index("c"),
            block_count[0],
            lax.axis_index("y"),
        ]
    ).astype(jnp.int32)
    pay = call(prep_kernel, shape((PAD, R), BF), (cell_factor, gene_factor), "vv", name="prep")
    g1 = gathered(pay)
    common = [pltpu.VMEM((NB, BLK, BLK), BF), pltpu.VMEM((genes, R), BF)]
    keep, send, gene_sums = call(
        cells_kernel,
        (shape((half, R), F32), shape((half, R), BF), shape((8, R), F32)),
        (meta, block_rows, block_cols, blocks, g1, gene_factor),
        "sssavv",
        common + [pltpu.VMEM((2 * half, R), F32), pltpu.SemaphoreType.DMA((NB,))],
        name="cells",
    )
    part = keep + shift(send, "c", 1).astype(F32)
    quarter = half // 4
    sent = [shift(part[k * quarter : (k + 1) * quarter].astype(BF), "x", k) for k in (1, 2, 3)]
    part = part[:quarter]
    for arrived in sent:
        part = part + arrived.astype(F32)
    own = part[:HALF]
    sent = [shift(part[k * HALF : (k + 1) * HALF], "zl", k) for k in (1, 2, 3)]
    cell_new, pay = call(
        update_kernel,
        (shape((HALF, R), F32), shape((PAD, R), BF)),
        (own, *sent, cell_factor, gene_sums),
        "vvvvvv",
        name="update",
    )
    g2 = gathered(pay)
    mine, send, cell_part = call(
        genes_kernel,
        (shape((BLK, R), F32), shape((3, BLK + 16, R), BF), shape((8, R), F32)),
        (meta, block_rows, block_cols, blocks, g2, gene_factor),
        "sssavv",
        common
        + [
            pltpu.VMEM((16, R, BLK), BF),
            pltpu.VMEM((4, R, BLK), F32),
            pltpu.SemaphoreType.DMA((NB,)),
        ],
        name="genes",
    )
    arrived = [shift(send[k - 1], "y", k) for k in (1, 2, 3)]
    folded = call(
        fold_kernel, shape((BLK + 8, R), F32), (mine, cell_part, *arrived), "vvvvv", name="fold"
    )
    other = shift(folded, "zh", 1)
    fresh = call(
        finish_kernel,
        shape((BLK, R), F32),
        (meta, folded, other, gene_factor),
        "svvv",
        name="finish",
    )
    parts = [fresh] + [shift(fresh, "y", k) for k in (1, 2, 3)]
    gene_new = call(
        place_kernel, shape((genes, R), F32), (meta, *parts), "svvvv", name="place"
    )
    return (cell_new, gene_new)


def solution(mesh):
    torus = Mesh(mesh.devices.reshape(4, 2, 4, 4, 2), CELL_GENE)
    return jax.shard_map(
        on_device,
        mesh=torus,
        in_specs=(
            P(CELL_GENE, None, None),
            P(CELL_GENE),
            P(CELL_GENE),
            P(CELL_GENE),
            P(CELL_GENE, None),
            P(GENE, None),
        ),
        out_specs=(P(CELL_GENE, None), P(GENE, None)),
        check_vma=False,
    )
```

```python
import jax
import jax.numpy as jnp
from jax import lax
from jax.experimental import pallas as pl
from jax.experimental.pallas import tpu as pltpu
from jax.sharding import Mesh
from jax.sharding import PartitionSpec as P

GENE = ("x", "zl", "c")
CELL_GENE = ("y", "zh", "x", "zl", "c")

BLK = 256
R = 128
NB = 48
HALF = 128
PAD = 144
UNITS = 32
GROUP = 16
BF = jnp.bfloat16
F32 = jnp.float32
NT = (((1,), (1,)), ((), ()))
TN = (((0,), (0,)), ((), ()))
VMEM_LIMIT = 24 * 1024 * 1024


SHIFTED = ('zl', 'y')


def partner(axis, i, step):
    return i + step if axis in SHIFTED else i ^ step


def swap(value, axis, step):
    count = lax.axis_size(axis)
    return lax.ppermute(value, axis, [(i, partner(axis, i, step) % count) for i in range(count)])


def gathered(payload):
    for axis in ("zl", "x", "c"):
        parts = [payload] + [swap(payload, axis, k) for k in range(1, lax.axis_size(axis))]
        payload = jnp.concatenate(parts, 0)
    return payload


def three_pieces(total):
    hi = total.astype(BF)
    rest = total - hi.astype(F32)
    mid = rest.astype(BF)
    lo = (rest - mid.astype(F32)).astype(BF)
    wide = lambda a: jnp.concatenate([a.astype(F32)] * 2, 0)
    which = lax.broadcasted_iota(jnp.int32, (16, R), 0)
    rows = jnp.where(
        which == 0,
        wide(hi),
        jnp.where(which == 1, wide(mid), jnp.where(which == 2, wide(lo), 0.0)),
    )
    return rows.astype(BF)


def column_sum(value):
    return jnp.broadcast_to(jnp.sum(value, 0, keepdims=True), (8, R))


def prep_kernel(cell_ref, gene_ref, pay_ref, hb_ref, cell, gene, sems):
    copies = [
        pltpu.make_async_copy(gene_ref, gene, sems.at[0]),
        pltpu.make_async_copy(cell_ref, cell, sems.at[1]),
    ]
    for copy in copies:
        copy.start()
    for copy in copies:
        copy.wait()
    pay_ref[:HALF, :] = cell[...].astype(BF)
    pay_ref[HALF:, :] = three_pieces(column_sum(gene[...]))
    hb_ref[...] = gene[...].astype(BF)


def slot_base(meta, row, other):
    dx = meta[0] ^ (row >> 2)
    dz = (meta[1] - (row & 3)) & 3
    return pl.multiple_of((other * 16 + dx * 4 + dz) * PAD, 16)


def unit_base(meta, row):
    dx = meta[0] ^ (row >> 2)
    dz = ((row & 3) - meta[1]) & 3
    return pl.multiple_of((dx * 4 + dz) * HALF, HALF)


def group_sum(g_ref):
    total = jnp.zeros((16, R), F32)
    for u in range(UNITS):
        total = total + g_ref[u * PAD + HALF : (u + 1) * PAD, :].astype(F32)
    return column_sum(total)


def ratio_of(tile, w, h, live):
    model = lax.dot_general(w, h, NT, preferred_element_type=F32)
    return jnp.where(live, tile.astype(F32) / model, 0.0).astype(BF)


def cells_kernel(
    meta, rows, cols, blocks_ref, g_ref, hb_ref, keep_ref, send_ref, sum_ref, acc, tiles, sems
):
    def batch(p):
        at = pl.ds(p * GROUP, GROUP)
        return pltpu.make_async_copy(blocks_ref.at[at], tiles.at[at], sems.at[p])

    for p in range(NB // GROUP):
        batch(p).start()
    keep_ref[...] = jnp.zeros_like(keep_ref)
    acc[...] = jnp.zeros_like(acc)
    sum_ref[...] = group_sum(g_ref)
    count = meta[3]

    def step(p, carry):
        batch(p).wait()
        found = []
        for k in range(GROUP):
            s = p * GROUP + k
            row = rows[s]
            h = hb_ref[pl.ds(pl.multiple_of(cols[s] * BLK, BLK), BLK), :]
            terms = []
            for other in (0, 1):
                w = g_ref[pl.ds(slot_base(meta, row, other), HALF), :]
                at = pl.multiple_of((meta[2] ^ other) * HALF, HALF)
                ratio = ratio_of(tiles[s, pl.ds(at, HALF), :], w, h, s < count)
                terms.append(jnp.dot(ratio, h, preferred_element_type=F32))
            found.append((unit_base(meta, row), terms))
        for at, terms in found:
            at = pl.ds(at, HALF)
            keep_ref[at, :] = keep_ref[at, :] + terms[0]
            acc[at, :] = acc[at, :] + terms[1]
        return carry

    steps = (count + GROUP - 1) // GROUP
    lax.fori_loop(0, steps, step, 0)
    send_ref[...] = acc[...].astype(BF)

    def drain(p, carry):
        batch(p).wait()
        return carry

    lax.fori_loop(steps, NB // GROUP, drain, 0)


def update_kernel(own_ref, r1_ref, r2_ref, r3_ref, cell_ref, sum_ref, new_ref, pay_ref):
    numer = own_ref[...] + r1_ref[...] + r2_ref[...] + r3_ref[...]
    new = cell_ref[...] * numer / sum_ref[0:1, :]
    new_ref[...] = new
    pay_ref[:HALF, :] = new.astype(BF)
    pay_ref[HALF:, :] = three_pieces(column_sum(new))


def genes_kernel(
    meta, rows, cols, blocks_ref, g_ref, hb_ref, own_ref, s1_ref, s2_ref, s3_ref, acc
):
    acc[...] = jnp.zeros_like(acc)
    total = group_sum(g_ref)
    count = meta[3]

    def step(p, carry):
        found = []
        for k in range(GROUP):
            s = p * GROUP + k
            row = rows[s]
            h = hb_ref[pl.ds(pl.multiple_of(cols[s] * BLK, BLK), BLK), :]
            w = jnp.concatenate(
                [
                    g_ref[pl.ds(slot_base(meta, row, meta[2] ^ parity), HALF), :]
                    for parity in (0, 1)
                ],
                0,
            )
            ratio = ratio_of(blocks_ref[s], w, h, s < count)
            found.append(
                (
                    (cols[s] - meta[4]) & 3,
                    lax.dot_general(ratio, w, TN, preferred_element_type=F32),
                )
            )
        for at, terms in found:
            acc[at] = acc[at] + terms
        return carry

    lax.fori_loop(0, (count + GROUP - 1) // GROUP, step, 0)
    for k, ref in enumerate((own_ref, s1_ref, s2_ref, s3_ref)):
        ref[:BLK, :] = acc[k]
        ref[BLK:, :] = total


def fold_kernel(own_ref, r1_ref, r2_ref, r3_ref, out_ref):
    out_ref[...] = own_ref[...] + r1_ref[...] + r2_ref[...] + r3_ref[...]


def finish_kernel(meta, mine_ref, other_ref, gene_ref, out_ref):
    both = mine_ref[...] + other_ref[...]
    at = pl.ds(pl.multiple_of(meta[4] * BLK, BLK), BLK)
    out_ref[...] = gene_ref[at, :] * both[:BLK] / both[BLK : BLK + 1]


def place_kernel(meta, p0_ref, p1_ref, p2_ref, p3_ref, out_ref, sems):
    copies = []
    for k, ref in enumerate((p0_ref, p1_ref, p2_ref, p3_ref)):
        at = pl.ds(pl.multiple_of(((meta[4] - k) & 3) * BLK, BLK), BLK)
        copies.append(pltpu.make_async_copy(ref, out_ref.at[at, :], sems.at[k]))
    for copy in copies:
        copy.start()
    for copy in copies:
        copy.wait()


def vspec():
    return pl.BlockSpec(memory_space=pltpu.VMEM)


def sspec():
    return pl.BlockSpec(memory_space=pltpu.SMEM)


def call(kernel, outs, args, kinds, gives="", scratch=(), name=None):
    spec = {"s": sspec, "v": vspec, "a": lambda: pl.BlockSpec(memory_space=pl.ANY)}
    kept = [spec[kind]() for kind in gives or "v" * len(jax.tree.leaves(outs))]
    return pl.pallas_call(
        kernel,
        out_shape=outs,
        in_specs=[spec[kind]() for kind in kinds],
        out_specs=tuple(kept) if isinstance(outs, tuple) else kept[0],
        scratch_shapes=list(scratch),
        name=name,
        compiler_params=pltpu.CompilerParams(vmem_limit_bytes=VMEM_LIMIT),
    )(*args)


def in_hbm(value):
    return pltpu.with_memory_space_constraint(value, pltpu.HBM)


def shape(dims, dtype):
    return jax.ShapeDtypeStruct(dims, dtype)


def on_device(blocks, block_rows, block_cols, block_count, cell_factor, gene_factor):
    genes = gene_factor.shape[0]
    half = UNITS // 2 * HALF
    meta = jnp.stack(
        [
            lax.axis_index("x"),
            lax.axis_index("zl"),
            lax.axis_index("c"),
            block_count[0],
            lax.axis_index("y"),
        ]
    ).astype(jnp.int32)
    pay, hb = call(
        prep_kernel,
        (shape((PAD, R), BF), shape((genes, R), BF)),
        (in_hbm(cell_factor), in_hbm(gene_factor)),
        "aa",
        scratch=[
            pltpu.VMEM((HALF, R), F32),
            pltpu.VMEM((genes, R), F32),
            pltpu.SemaphoreType.DMA((2,)),
        ],
        name="prep",
    )
    g1 = gathered(pay)
    keep, send, gene_sums = call(
        cells_kernel,
        (shape((half, R), F32), shape((half, R), BF), shape((8, R), F32)),
        (meta, block_rows, block_cols, in_hbm(blocks), g1, hb),
        "sssavv",
        scratch=[
            pltpu.VMEM((half, R), F32),
            pltpu.VMEM((NB, BLK, BLK), BF),
            pltpu.SemaphoreType.DMA((NB // GROUP,)),
        ],
        name="cells",
    )
    part = keep + swap(send, "c", 1).astype(F32)
    quarter = half // 4
    sent = [swap(part[k * quarter : (k + 1) * quarter].astype(BF), "x", k) for k in (1, 2, 3)]
    part = part[:quarter]
    for arrived in sent:
        part = part + arrived.astype(F32)
    own = part[:HALF]
    sent = [swap(part[k * HALF : (k + 1) * HALF], "zl", k) for k in (1, 2, 3)]
    cell_new, pay = call(
        update_kernel,
        (shape((HALF, R), F32), shape((PAD, R), BF)),
        (own, *sent, cell_factor, gene_sums),
        "vvvvvv",
        name="update",
    )
    g2 = gathered(pay)
    mine, *send = call(
        genes_kernel,
        (shape((BLK + 8, R), F32),) * 4,
        (meta, block_rows, block_cols, blocks, g2, hb),
        "sssvvv",
        scratch=[pltpu.VMEM((4, BLK, R), F32)],
        name="genes",
    )
    arrived = [swap(send[k - 1], "y", k) for k in (1, 2, 3)]
    folded = call(fold_kernel, shape((BLK + 8, R), F32), (mine, *arrived), "vvvv", name="fold")
    other = swap(folded, "zh", 1)
    fresh = call(
        finish_kernel,
        shape((BLK, R), F32),
        (meta, folded, other, gene_factor),
        "svvv",
        name="finish",
    )
    parts = [fresh] + [swap(fresh, "y", k) for k in (1, 2, 3)]
    gene_new = call(
        place_kernel,
        shape((genes, R), F32),
        (meta, *parts),
        "svvvv",
        gives="a",
        scratch=[pltpu.SemaphoreType.DMA((4,))],
        name="place",
    )
    return (cell_new, gene_new)


def solution(mesh):
    torus = Mesh(mesh.devices.reshape(4, 2, 4, 4, 2), CELL_GENE)
    return jax.shard_map(
        on_device,
        mesh=torus,
        in_specs=(
            P(CELL_GENE, None, None),
            P(CELL_GENE),
            P(CELL_GENE),
            P(CELL_GENE),
            P(CELL_GENE, None),
            P(GENE, None),
        ),
        out_specs=(P(CELL_GENE, None), P(GENE, None)),
        check_vma=False,
    )
```

```python
import jax
import jax.numpy as jnp
from jax import lax
from jax.experimental import pallas as pl
from jax.experimental.pallas import tpu as pltpu
from jax.sharding import Mesh
from jax.sharding import PartitionSpec as P

GENE = ("x", "zl", "c")
CELL_GENE = ("y", "zh", "x", "zl", "c")

BLK = 256
R = 128
NB = 48
HALF = 128
PAD = 144
UNITS = 32
GROUP = 16
BF = jnp.bfloat16
F32 = jnp.float32
NT = (((1,), (1,)), ((), ()))
TN = (((0,), (0,)), ((), ()))
VMEM_LIMIT = 24 * 1024 * 1024


SHIFTED = ('zl', 'y')


def partner(axis, i, step):
    if axis == "zl":
        return label((label(i) + step) % 4)
    return i + step if axis in SHIFTED else i ^ step


def label(i):
    return i ^ (i >> 1)


def swap(value, axis, step):
    count = lax.axis_size(axis)
    return lax.ppermute(value, axis, [(i, partner(axis, i, step) % count) for i in range(count)])


def gathered(payload):
    for axis in ("zl", "x", "c"):
        parts = [payload] + [swap(payload, axis, k) for k in range(1, lax.axis_size(axis))]
        payload = jnp.concatenate(parts, 0)
    return payload


def three_pieces(total):
    hi = total.astype(BF)
    rest = total - hi.astype(F32)
    mid = rest.astype(BF)
    lo = (rest - mid.astype(F32)).astype(BF)
    wide = lambda a: jnp.concatenate([a.astype(F32)] * 2, 0)
    which = lax.broadcasted_iota(jnp.int32, (16, R), 0)
    rows = jnp.where(
        which == 0,
        wide(hi),
        jnp.where(which == 1, wide(mid), jnp.where(which == 2, wide(lo), 0.0)),
    )
    return rows.astype(BF)


def column_sum(value):
    return jnp.broadcast_to(jnp.sum(value, 0, keepdims=True), (8, R))


def prep_kernel(cell_ref, gene_ref, pay_ref, hb_ref, cell, gene, sems):
    copies = [
        pltpu.make_async_copy(gene_ref, gene, sems.at[0]),
        pltpu.make_async_copy(cell_ref, cell, sems.at[1]),
    ]
    for copy in copies:
        copy.start()
    for copy in copies:
        copy.wait()
    pay_ref[:HALF, :] = cell[...].astype(BF)
    pay_ref[HALF:, :] = three_pieces(column_sum(gene[...]))
    hb_ref[...] = gene[...].astype(BF)


def slot_base(meta, row, other):
    dx = meta[0] ^ (row >> 2)
    dz = (label(meta[1]) - label(row & 3)) & 3
    return pl.multiple_of((other * 16 + dx * 4 + dz) * PAD, 16)


def unit_base(meta, row):
    dx = meta[0] ^ (row >> 2)
    dz = (label(row & 3) - label(meta[1])) & 3
    return pl.multiple_of((dx * 4 + dz) * HALF, HALF)


def group_sum(g_ref):
    total = jnp.zeros((16, R), F32)
    for u in range(UNITS):
        total = total + g_ref[u * PAD + HALF : (u + 1) * PAD, :].astype(F32)
    return column_sum(total)


def ratio_of(tile, w, h, live):
    model = lax.dot_general(w, h, NT, preferred_element_type=F32)
    return jnp.where(live, tile.astype(F32) / model, 0.0).astype(BF)


def cells_kernel(
    meta, rows, cols, blocks_ref, g_ref, hb_ref, keep_ref, send_ref, sum_ref, acc, tiles, sems
):
    def batch(p):
        at = pl.ds(p * GROUP, GROUP)
        return pltpu.make_async_copy(blocks_ref.at[at], tiles.at[at], sems.at[p])

    for p in range(NB // GROUP):
        batch(p).start()
    keep_ref[...] = jnp.zeros_like(keep_ref)
    acc[...] = jnp.zeros_like(acc)
    sum_ref[...] = group_sum(g_ref)
    count = meta[3]

    def step(p, carry):
        batch(p).wait()
        found = []
        for k in range(GROUP):
            s = p * GROUP + k
            row = rows[s]
            h = hb_ref[pl.ds(pl.multiple_of(cols[s] * BLK, BLK), BLK), :]
            terms = []
            for other in (0, 1):
                w = g_ref[pl.ds(slot_base(meta, row, other), HALF), :]
                at = pl.multiple_of((meta[2] ^ other) * HALF, HALF)
                ratio = ratio_of(tiles[s, pl.ds(at, HALF), :], w, h, s < count)
                terms.append(jnp.dot(ratio, h, preferred_element_type=F32))
            found.append((unit_base(meta, row), terms))
        for at, terms in found:
            at = pl.ds(at, HALF)
            keep_ref[at, :] = keep_ref[at, :] + terms[0]
            acc[at, :] = acc[at, :] + terms[1]
        return carry

    steps = (count + GROUP - 1) // GROUP
    lax.fori_loop(0, steps, step, 0)
    send_ref[...] = acc[...].astype(BF)

    def drain(p, carry):
        batch(p).wait()
        return carry

    lax.fori_loop(steps, NB // GROUP, drain, 0)


def update_kernel(own_ref, r1_ref, r2_ref, r3_ref, cell_ref, sum_ref, new_ref, pay_ref):
    numer = own_ref[...] + r1_ref[...] + r2_ref[...] + r3_ref[...]
    new = cell_ref[...] * numer / sum_ref[0:1, :]
    new_ref[...] = new
    pay_ref[:HALF, :] = new.astype(BF)
    pay_ref[HALF:, :] = three_pieces(column_sum(new))


def genes_kernel(
    meta,
    rows,
    cols,
    blocks_ref,
    g_ref,
    hb_ref,
    new_ref,
    own_ref,
    s1_ref,
    s2_ref,
    s3_ref,
    out_ref,
    acc,
    sem,
):
    leaving = pltpu.make_async_copy(new_ref, out_ref, sem)
    leaving.start()
    acc[...] = jnp.zeros_like(acc)
    total = group_sum(g_ref)
    count = meta[3]

    def step(p, carry):
        found = []
        for k in range(GROUP):
            s = p * GROUP + k
            row = rows[s]
            h = hb_ref[pl.ds(pl.multiple_of(cols[s] * BLK, BLK), BLK), :]
            w = jnp.concatenate(
                [
                    g_ref[pl.ds(slot_base(meta, row, meta[2] ^ parity), HALF), :]
                    for parity in (0, 1)
                ],
                0,
            )
            ratio = ratio_of(blocks_ref[s], w, h, s < count)
            found.append(
                (
                    (cols[s] - meta[4]) & 3,
                    lax.dot_general(ratio, w, TN, preferred_element_type=F32),
                )
            )
        for at, terms in found:
            acc[at] = acc[at] + terms
        return carry

    lax.fori_loop(0, (count + GROUP - 1) // GROUP, step, 0)
    for k, ref in enumerate((own_ref, s1_ref, s2_ref, s3_ref)):
        ref[:BLK, :] = acc[k]
        ref[BLK:, :] = total
    leaving.wait()


def fold_kernel(own_ref, r1_ref, r2_ref, r3_ref, out_ref):
    out_ref[...] = own_ref[...] + r1_ref[...] + r2_ref[...] + r3_ref[...]


def place_kernel(meta, gene_ref, p0_ref, p1_ref, p2_ref, p3_ref, out_ref, fresh, sems):
    copies = []
    for k, ref in enumerate((p0_ref, p1_ref, p2_ref, p3_ref)):
        at = pl.ds(pl.multiple_of(((meta[4] - k) & 3) * BLK, BLK), BLK)
        fresh[k] = gene_ref[at, :] * ref[:BLK, :] / ref[BLK : BLK + 1, :]
        copies.append(pltpu.make_async_copy(fresh.at[k], out_ref.at[at, :], sems.at[k]))
        copies[k].start()
    for copy in copies:
        copy.wait()


def vspec():
    return pl.BlockSpec(memory_space=pltpu.VMEM)


def sspec():
    return pl.BlockSpec(memory_space=pltpu.SMEM)


def call(kernel, outs, args, kinds, gives="", scratch=(), name=None):
    spec = {"s": sspec, "v": vspec, "a": lambda: pl.BlockSpec(memory_space=pl.ANY)}
    kept = [spec[kind]() for kind in gives or "v" * len(jax.tree.leaves(outs))]
    return pl.pallas_call(
        kernel,
        out_shape=outs,
        in_specs=[spec[kind]() for kind in kinds],
        out_specs=tuple(kept) if isinstance(outs, tuple) else kept[0],
        scratch_shapes=list(scratch),
        name=name,
        compiler_params=pltpu.CompilerParams(vmem_limit_bytes=VMEM_LIMIT),
    )(*args)


def in_hbm(value):
    return pltpu.with_memory_space_constraint(value, pltpu.HBM)


def shape(dims, dtype):
    return jax.ShapeDtypeStruct(dims, dtype)


def on_device(blocks, block_rows, block_cols, block_count, cell_factor, gene_factor):
    genes = gene_factor.shape[0]
    half = UNITS // 2 * HALF
    meta = jnp.stack(
        [
            lax.axis_index("x"),
            lax.axis_index("zl"),
            lax.axis_index("c"),
            block_count[0],
            lax.axis_index("y"),
        ]
    ).astype(jnp.int32)
    pay, hb = call(
        prep_kernel,
        (shape((PAD, R), BF), shape((genes, R), BF)),
        (in_hbm(cell_factor), in_hbm(gene_factor)),
        "aa",
        scratch=[
            pltpu.VMEM((HALF, R), F32),
            pltpu.VMEM((genes, R), F32),
            pltpu.SemaphoreType.DMA((2,)),
        ],
        name="prep",
    )
    g1 = gathered(pay)
    keep, send, gene_sums = call(
        cells_kernel,
        (shape((half, R), F32), shape((half, R), BF), shape((8, R), F32)),
        (meta, block_rows, block_cols, in_hbm(blocks), g1, hb),
        "sssavv",
        scratch=[
            pltpu.VMEM((half, R), F32),
            pltpu.VMEM((NB, BLK, BLK), BF),
            pltpu.SemaphoreType.DMA((NB // GROUP,)),
        ],
        name="cells",
    )
    part = keep + swap(send, "c", 1).astype(F32)
    quarter = half // 4
    sent = [swap(part[k * quarter : (k + 1) * quarter].astype(BF), "x", k) for k in (1, 2, 3)]
    part = part[:quarter]
    for arrived in sent:
        part = part + arrived.astype(F32)
    own = part[:HALF]
    sent = [swap(part[k * HALF : (k + 1) * HALF], "zl", k) for k in (1, 2, 3)]
    fresh, pay = call(
        update_kernel,
        (shape((HALF, R), F32), shape((PAD, R), BF)),
        (own, *sent, cell_factor, gene_sums),
        "vvvvvv",
        name="update",
    )
    g2 = gathered(pay)
    mine, *send, cell_new = call(
        genes_kernel,
        (shape((BLK + 8, R), F32),) * 4 + (shape((HALF, R), F32),),
        (meta, block_rows, block_cols, blocks, g2, hb, fresh),
        "sssvvvv",
        gives="vvvva",
        scratch=[pltpu.VMEM((4, BLK, R), F32), pltpu.SemaphoreType.DMA],
        name="genes",
    )
    arrived = [swap(send[k - 1], "y", k) for k in (1, 2, 3)]
    folded = call(fold_kernel, shape((BLK + 8, R), F32), (mine, *arrived), "vvvv", name="fold")
    both = folded + swap(folded, "zh", 1)
    parts = [both] + [swap(both, "y", k) for k in (1, 2, 3)]
    gene_new = call(
        place_kernel,
        shape((genes, R), F32),
        (meta, gene_factor, *parts),
        "svvvvv",
        gives="a",
        scratch=[pltpu.VMEM((4, BLK, R), F32), pltpu.SemaphoreType.DMA((4,))],
        name="place",
    )
    return (cell_new, gene_new)


def solution(mesh):
    torus = Mesh(mesh.devices.reshape(4, 2, 4, 4, 2), CELL_GENE)
    return jax.shard_map(
        on_device,
        mesh=torus,
        in_specs=(
            P(CELL_GENE, None, None),
            P(CELL_GENE),
            P(CELL_GENE),
            P(CELL_GENE),
            P(CELL_GENE, None),
            P(GENE, None),
        ),
        out_specs=(P(CELL_GENE, None), P(GENE, None)),
        check_vma=False,
    )
```
